256 devices in a mesh: rows: 8 (over z_hi, core), cols: 32 (over x, y, z_lo).
Axes of the slice: x: 4, y: 4, z: 8 (z_hi: 4, z_lo: 2; z = z_hi * 2 + z_lo), core: 2. Of those that a mesh axis runs over, the one named last changes fastest.
Arguments:
- covariance: float32 [16384, 16384], P('rows', 'cols'), may hold values from -0.5 to 9.5, as said below
- prior_concentration: float32 [16384], replicated, may hold values from -6 to 6
- east_wind: float32 [64, 256], replicated, may hold values from -0.35 to 0.35
- north_wind: float32 [64, 256], replicated, may hold values from -0.35 to 0.35
- diffusivity: float32 [64, 256], replicated, may hold values from 0.02 to 0.07
- sensor_cell_position: int32 [128, 16], replicated, may hold values from 0 to 16383, as said below
- sensor_cell_share: float32 [128, 16], replicated, may hold values from 0.1 to 0.4
- measurement_readings: float32 [128], replicated, may hold values from -6 to 6
- obs_variance: float32 [128], replicated, may hold values from 0.2 to 2
Outputs:
- cov_analysis: float32 [16384, 16384], P('rows', 'cols')
- corrected_concentration: float32 [16384], P('rows')
The draws below stay inside these ranges and needn't reach their ends.
Inputs may be any that keep to these rules, and one draw needn't show every extreme that they name: `covariance`: symmetric and positive definite. `sensor_cell_position`: the 16 indices of an observation are the cells of a 4 x 4 patch of neighbouring latitudes and longitudes (longitudes wrap), index = latitude * 256 + longitude.
All inputs are finite; a program needn't handle non-finite values.
Results may differ from the reference program's by a relative error of at most 0.00011.
Values sent between devices are 32-bit elements; how exact they have to be, the bound alone decides.
No kernel may reach another device: no remote copies, remote signals or barrier semaphores. Data moves between devices by JAX's collectives and lax.ppermute only.
A program may use at most 128 MiB of HBM per device.

```python
import math
import jax
import jax.numpy as jnp
from jax import lax

LAT = 64
MERIDIAN_NUMBER = 256
OBS = 128
FOOT_SIDE = 4
FP = 16
GRID_CELL_NUMBER = 16384


def draw_covariance(key, part):
    subkeys = jax.random.split(jax.random.fold_in(key, 17), 2)
    entries = jax.random.normal(subkeys[0], (GRID_CELL_NUMBER, GRID_CELL_NUMBER), jnp.float32)
    scales = jnp.exp(jax.random.uniform(subkeys[1], (GRID_CELL_NUMBER,), jnp.float32, math.log(0.5), math.log(2.0)))
    symmetric = (entries + entries.T) * (0.25 / math.sqrt(2.0 * GRID_CELL_NUMBER))
    correlation = symmetric + jnp.eye(GRID_CELL_NUMBER, dtype=jnp.float32)
    return scales[:, None] * correlation * scales[None, :]


def draw_sensor_cell_position(key, part):
    subkeys = jax.random.split(jax.random.fold_in(key, 29), 2)
    first_lat = jax.random.randint(subkeys[0], (OBS, 1), 0, LAT - FOOT_SIDE + 1)
    first_lon = jax.random.randint(subkeys[1], (OBS, 1), 0, MERIDIAN_NUMBER)
    offsets = jnp.arange(FP, dtype=jnp.int32)[None, :]
    latitude = first_lat + offsets // FOOT_SIDE
    longitude = (first_lon + offsets % FOOT_SIDE) % MERIDIAN_NUMBER
    return (latitude * MERIDIAN_NUMBER + longitude).astype(jnp.int32)


def scatter_about(key, shape, width, bound, kind=jnp.bfloat16):
    return jnp.clip(width * jax.random.normal(key, shape, jnp.float32), -bound, bound).astype(kind)


def setup_inputs(seed: int = 0) -> dict:
    keys = jax.random.split(jax.random.key(seed), 10)
    covariance = draw_covariance(jax.random.fold_in(keys[9], 71), 0)
    prior_concentration = scatter_about(keys[1], (GRID_CELL_NUMBER,), 1.0, 6.0, jnp.float32)
    east_wind = jnp.clip(jax.random.uniform(keys[2], (LAT, MERIDIAN_NUMBER), jnp.float32, -0.35, 0.35), -0.35, 0.35)
    north_wind = jnp.clip(jax.random.uniform(keys[3], (LAT, MERIDIAN_NUMBER), jnp.float32, -0.35, 0.35), -0.35, 0.35)
    diffusivity = jnp.clip(jnp.exp(jax.random.uniform(keys[4], (LAT, MERIDIAN_NUMBER), jnp.float32, math.log(0.02), math.log(0.07))), 0.02, 0.07)
    sensor_cell_position = draw_sensor_cell_position(jax.random.fold_in(keys[9], 71), 0)
    sensor_cell_share = jnp.clip(jax.random.uniform(keys[6], (OBS, FP), jnp.float32, 0.1, 0.4), 0.1, 0.4)
    measurement_readings = scatter_about(keys[7], (OBS,), 1.0, 6.0, jnp.float32)
    obs_variance = jnp.clip(jnp.exp(jax.random.uniform(keys[8], (OBS,), jnp.float32, math.log(0.2), math.log(2.0))), 0.2, 2.0)
    return dict(covariance=covariance, prior_concentration=prior_concentration, east_wind=east_wind, north_wind=north_wind, diffusivity=diffusivity, sensor_cell_position=sensor_cell_position, sensor_cell_share=sensor_cell_share, measurement_readings=measurement_readings, obs_variance=obs_variance)


def coefficients(east_wind, north_wind, diffusivity):
    western = jnp.maximum(east_wind, 0.0) + diffusivity
    eastern = jnp.maximum(-east_wind, 0.0) + diffusivity
    southern = jnp.maximum(north_wind, 0.0) + diffusivity
    northern = jnp.maximum(-north_wind, 0.0) + diffusivity
    middle = 1.0 - (western + eastern + southern + northern)
    return (middle, western, eastern, southern, northern)

def advance_step(extended, neighbour_coefficients, lat_axis):
    count = extended.shape[lat_axis] - 2
    middle = lax.slice_in_dim(extended, 1, count + 1, axis=lat_axis)
    southern = lax.slice_in_dim(extended, 0, count, axis=lat_axis)
    northern = lax.slice_in_dim(extended, 2, count + 2, axis=lat_axis)
    western = jnp.roll(middle, 1, axis=lat_axis + 1)
    eastern = jnp.roll(middle, -1, axis=lat_axis + 1)
    return neighbour_coefficients[0] * middle + neighbour_coefficients[1] * western + neighbour_coefficients[2] * eastern + neighbour_coefficients[3] * southern + neighbour_coefficients[4] * northern

def padded_step(mapped_cell_numbers, neighbour_coefficients, lat_axis):
    widths = [(0, 0)] * mapped_cell_numbers.ndim
    widths[lat_axis] = (1, 1)
    return advance_step(jnp.pad(mapped_cell_numbers, widths), neighbour_coefficients, lat_axis)

def footprint_matrix(sensor_cell_position, sensor_cell_share, start, count):
    positions = start + jnp.arange(count, dtype=jnp.int32)

    def accumulate(footpoint, running):
        picked = lax.dynamic_slice_in_dim(sensor_cell_position, footpoint, 1, 1)
        weights = lax.dynamic_slice_in_dim(sensor_cell_share, footpoint, 1, 1)
        return running + weights * (picked == positions[None, :]).astype(jnp.float32)
    return lax.fori_loop(0, sensor_cell_position.shape[1], accumulate, jnp.zeros((sensor_cell_position.shape[0], count), jnp.float32))

def expected_average(prior_concentration, neighbour_coefficients, longitude_total):
    mapped_cell_numbers = prior_concentration.reshape(-1, longitude_total)
    for section_index in range(2):
        mapped_cell_numbers = padded_step(mapped_cell_numbers, neighbour_coefficients, 0)
    return mapped_cell_numbers.reshape(-1)

def cholesky_solve(matrix, right_sides):
    lower = jnp.linalg.cholesky(matrix)
    halfway = lax.linalg.triangular_solve(lower, right_sides, left_side=True, lower=True)
    return lax.linalg.triangular_solve(lower, halfway, left_side=True, lower=True, transpose_a=True)

def reference(covariance, prior_concentration, east_wind, north_wind, diffusivity, sensor_cell_position, sensor_cell_share, measurement_readings, obs_variance):
    highest_accuracy_mode = lax.Precision.HIGHEST
    neighbour_coefficients = coefficients(east_wind, north_wind, diffusivity)
    row_coefs = tuple((member[:, :, None] for member in neighbour_coefficients))
    col_coefs = tuple((member[None, :, :] for member in neighbour_coefficients))
    blocked_concentration = covariance.reshape(LAT, MERIDIAN_NUMBER, GRID_CELL_NUMBER)
    for section_index in range(2):
        blocked_concentration = padded_step(blocked_concentration, row_coefs, 0)
    blocked_concentration = blocked_concentration.reshape(GRID_CELL_NUMBER, LAT, MERIDIAN_NUMBER)
    for section_index in range(2):
        blocked_concentration = padded_step(blocked_concentration, col_coefs, 1)
    prior_spread_matrix = blocked_concentration.reshape(GRID_CELL_NUMBER, GRID_CELL_NUMBER)
    propagated_concentration = expected_average(prior_concentration, neighbour_coefficients, MERIDIAN_NUMBER)
    measurement_mapping = footprint_matrix(sensor_cell_position, sensor_cell_share, 0, GRID_CELL_NUMBER)
    measured_spread_matrix = jnp.dot(measurement_mapping, prior_spread_matrix, precision=highest_accuracy_mode)
    joint_spread_matrix = jnp.dot(prior_spread_matrix, measurement_mapping.T, precision=highest_accuracy_mode)
    gram = jnp.dot(measured_spread_matrix, measurement_mapping.T, precision=highest_accuracy_mode)
    innovation_cov = gram + jnp.diag(obs_variance)
    misfit_residual = measurement_readings - jnp.sum(sensor_cell_share * propagated_concentration[sensor_cell_position], axis=1)
    blending_matrix_lines = cholesky_solve(innovation_cov, joint_spread_matrix.T)
    corrected_concentration = propagated_concentration + jnp.dot(misfit_residual, blending_matrix_lines, precision=highest_accuracy_mode)
    corrected_increment = lax.dot_general(blending_matrix_lines, measured_spread_matrix, (((0,), (0,)), ((), ())), precision=highest_accuracy_mode)
    return (prior_spread_matrix - corrected_increment, corrected_concentration)
```

```python
import functools

import jax
import jax.numpy as jnp
from jax import lax
from jax.experimental import pallas as pl
from jax.experimental.pallas import tpu as pltpu
from jax.sharding import PartitionSpec as P

HI = lax.Precision.HIGHEST
LON = 256
OBS = 128


def coefficients(east_wind, north_wind, diffusivity):
    western = jnp.maximum(east_wind, 0.0) + diffusivity
    eastern = jnp.maximum(-east_wind, 0.0) + diffusivity
    southern = jnp.maximum(north_wind, 0.0) + diffusivity
    northern = jnp.maximum(-north_wind, 0.0) + diffusivity
    middle = 1.0 - (western + eastern + southern + northern)
    return (middle, western, eastern, southern, northern)


def row_kernel(lats, n, off, outs, *refs):
    parts, coef = refs[: len(lats)], refs[len(lats)]
    out_refs = refs[len(lats) + 1 : len(lats) + 1 + len(outs)]
    wide, mid = refs[len(lats) + 1 + len(outs) :]

    @pl.when(pl.program_id(0) == 0)
    def _():
        for k in range(5):
            for j in range(n + 2):
                column = coef[(off + j) * LON : (off + j + 1) * LON, k : k + 1]
                wide[k, j] = jnp.broadcast_to(column, (LON, 128))

    def source(i):
        for ref, (first, count) in zip(parts, lats):
            if i < count:
                return ref[(first + i) * LON : (first + i + 1) * LON, :]
            i -= count

    def step(j, here, south, north):
        west = pltpu.roll(here, 1, axis=0)
        east = pltpu.roll(here, LON - 1, axis=0)
        return (
            wide[0, j] * here
            + wide[1, j] * west
            + wide[2, j] * east
            + wide[3, j] * south
            + wide[4, j] * north
        )

    for j in range(n + 2):
        mid[j] = step(j, source(j + 1), source(j), source(j + 2))
    at = 0
    for ref, count in zip(out_refs, outs):
        for i in range(count):
            j = at + 1
            ref[i * LON : (i + 1) * LON, :] = step(j, mid[j], mid[j - 1], mid[j + 1])
            at += 1


def row_step(parts, coef, off, outs):
    n = sum(outs)
    cols = parts[0][0].shape[1]
    lats = [(first, count) for _, first, count in parts]
    assert sum(count for _, count in lats) == n + 4
    rows = sum(a.shape[0] for a, _, _ in parts)
    return pl.pallas_call(
        functools.partial(row_kernel, lats, n, off, outs),
        grid=(cols // 128,),
        in_specs=[pl.BlockSpec((a.shape[0], 128), lambda i: (0, i)) for a, _, _ in parts]
        + [pl.BlockSpec(coef.shape, lambda i: (0, 0))],
        out_specs=[pl.BlockSpec((count * LON, 128), lambda i: (0, i)) for count in outs],
        out_shape=[jax.ShapeDtypeStruct((count * LON, cols), jnp.float32) for count in outs],
        scratch_shapes=[
            pltpu.VMEM((5, n + 2, LON, 128), jnp.float32),
            pltpu.VMEM((n + 2, LON, 128), jnp.float32),
        ],
        compiler_params=pltpu.CompilerParams(vmem_limit_bytes=40 << 20),
        cost_estimate=pl.CostEstimate(
            flops=20 * n * LON * cols, bytes_accessed=4 * cols * (rows + n * LON), transcendentals=0
        ),
        name="row_step",
    )(*[a for a, _, _ in parts], coef)


TILE = 16


def column_kernel(block, flag, own, swapped, passed, coef, left, right, *rest):
    out, product = rest[-2:]
    product[...] = jnp.dot(
        left[...], right[...], precision=HI, preferred_element_type=jnp.float32
    )
    low_bit = flag[0]

    def step(j, here, south, north):
        west = pltpu.roll(here, 1, axis=1)
        east = pltpu.roll(here, LON - 1, axis=1)
        c = [jnp.broadcast_to(coef[5 * j + k : 5 * j + k + 1, :], here.shape) for k in range(5)]
        return c[0] * here + c[1] * west + c[2] * east + c[3] * south + c[4] * north

    def tile(t, carry):
        at = pl.ds(pl.multiple_of(t * TILE, TILE), TILE)
        mine, near, far = own[at, :], swapped[at, :], passed[at, :]
        below = jnp.where(low_bit == 0, far, near)
        above = jnp.where(low_bit == 0, near, far)
        f = [below[:, :LON], below[:, LON:], mine[:, :LON], mine[:, LON:], above[:, :LON], above[:, LON:]]
        g = [step(j, f[j + 1], f[j], f[j + 2]) for j in range(4)]
        out[at, :LON] = step(1, g[1], g[0], g[2]) - product[at, :LON]
        out[at, LON:] = step(2, g[2], g[1], g[3]) - product[at, LON:]
        return carry

    lax.fori_loop(0, block // TILE, tile, 0)


def column_step(flag, own, swapped, passed, coef, left, right, first_lat, into):
    rows = own.shape[0]
    block = min(rows, 256)
    base = first_lat * LON // block
    spec = pl.BlockSpec((block, 2 * LON), lambda i: (i, 0))
    aliased = [] if into is None else [into]
    return pl.pallas_call(
        functools.partial(column_kernel, block),
        grid=(rows // block,),
        in_specs=[
            pl.BlockSpec(memory_space=pltpu.SMEM),
            spec,
            spec,
            spec,
            pl.BlockSpec(coef.shape, lambda i: (0, 0)),
            pl.BlockSpec((block, OBS), lambda i: (base + i, 0)),
            pl.BlockSpec(right.shape, lambda i: (0, 0)),
        ]
        + [pl.BlockSpec(memory_space=pl.ANY)] * len(aliased),
        out_specs=pl.BlockSpec((block, 2 * LON), lambda i: (base + i, 0)),
        out_shape=jax.ShapeDtypeStruct((8 * LON, 2 * LON), jnp.float32),
        scratch_shapes=[pltpu.VMEM((block, 2 * LON), jnp.float32)],
        input_output_aliases={7: 0} if aliased else {},
        compiler_params=pltpu.CompilerParams(vmem_limit_bytes=40 << 20),
        cost_estimate=pl.CostEstimate(
            flops=rows * 512 * 300, bytes_accessed=4 * rows * 512 * 4, transcendentals=0
        ),
        name="column_step",
    )(flag, own, swapped, passed, coef, left, right, *aliased)


def adjoint_kernel(n, start, position, share, coef, out, first, second):
    lane = lax.broadcasted_iota(jnp.int32, (OBS, LON), 1)
    for i in range(n + 4):
        base = start[0] + i * LON
        total = jnp.zeros((OBS, LON), jnp.float32)
        for f in range(position.shape[1]):
            hit = (position[:, f : f + 1] - base) == lane
            total = total + jnp.where(hit, share[:, f : f + 1], 0.0)
        first[i] = total

    def adjoint(field, i):
        def c(k, j):
            return coef[k * (n + 4) + j : k * (n + 4) + j + 1, :]

        here = field[i]
        return (
            c(0, i) * here
            + pltpu.roll(c(1, i) * here, LON - 1, axis=1)
            + pltpu.roll(c(2, i) * here, 1, axis=1)
            + c(3, i + 1) * field[i + 1]
            + c(4, i - 1) * field[i - 1]
        )

    for i in range(1, n + 3):
        second[i] = adjoint(first, i)
    for i in range(2, n + 2):
        out[:, (i - 2) * LON : (i - 1) * LON] = adjoint(second, i)


def adjoint_footprints(start, position, share, coef, n):
    vmem = pl.BlockSpec(memory_space=pltpu.VMEM)
    return pl.pallas_call(
        functools.partial(adjoint_kernel, n),
        in_specs=[pl.BlockSpec(memory_space=pltpu.SMEM), vmem, vmem, vmem],
        out_specs=vmem,
        out_shape=jax.ShapeDtypeStruct((OBS, n * LON), jnp.float32),
        scratch_shapes=[pltpu.VMEM((n + 4, OBS, LON), jnp.float32)] * 2,
        compiler_params=pltpu.CompilerParams(vmem_limit_bytes=40 << 20),
        cost_estimate=pl.CostEstimate(
            flops=OBS * LON * (n + 4) * 60, bytes_accessed=4 * OBS * LON * n, transcendentals=0
        ),
        name="adjoint_footprints",
    )(start, position, share, coef)


def cholesky_solve(matrix, right_sides):
    lower = jnp.linalg.cholesky(matrix)
    halfway = lax.linalg.triangular_solve(lower, right_sides, left_side=True, lower=True)
    return lax.linalg.triangular_solve(lower, halfway, left_side=True, lower=True, transpose_a=True)


def shards(
    covariance,
    prior_concentration,
    east_wind,
    north_wind,
    diffusivity,
    sensor_cell_position,
    sensor_cell_share,
    measurement_readings,
    obs_variance,
):
    rows_n, cols_n = lax.axis_size("rows"), lax.axis_size("cols")
    r, c = lax.axis_index("rows"), lax.axis_index("cols")
    up = [(i, i + 1) for i in range(rows_n - 1)]
    down = [(j, i) for i, j in up]
    swap = [(i, i ^ 1) for i in range(cols_n)]
    onward = [(i, i + 2) for i in range(0, cols_n - 2, 2)]
    onward += [(i, i - 2) for i in range(3, cols_n, 2)]
    planes = [[2 * i + k for i in range(cols_n // 2)] for k in range(2)]

    from_below = lax.ppermute(covariance[6 * LON :], "rows", up)
    from_above = lax.ppermute(covariance[: 2 * LON], "rows", down)

    coefs = coefficients(east_wind, north_wind, diffusivity)
    padded = jnp.pad(jnp.stack(coefs), ((0, 0), (2, 2), (0, 0)))
    row_band = lax.dynamic_slice_in_dim(padded, 8 * r, 12, 1)
    col_band = lax.dynamic_slice_in_dim(padded, 2 * c, 6, 1)
    down_coef = jnp.pad(row_band[:, 1:11].reshape(5, 10 * LON).T, ((0, 0), (0, 3)))
    across_coef = jnp.pad(col_band[:, 1:5].transpose(1, 0, 2).reshape(20, LON), ((0, 4), (0, 0)))

    inner = row_step([(covariance, 0, 8)], down_coef, 2, (2, 2))

    col_start = (2 * c - 2) * LON
    row_start = (8 * r - 2) * LON
    g_col = adjoint_footprints(
        col_start[None], sensor_cell_position, sensor_cell_share, col_band.reshape(30, LON), 2
    )
    g_row = adjoint_footprints(
        row_start[None], sensor_cell_position, sensor_cell_share, row_band.reshape(60, LON), 8
    )
    w_part = lax.dot_general(covariance, g_col, (((1,), (1,)), ((), ())), precision=HI)
    arrived = lax.all_to_all(
        w_part.reshape(16, 128, OBS), "cols", 0, 0, axis_index_groups=planes, tiled=True
    )
    piece = arrived.sum(axis=0)
    piece = piece + lax.ppermute(piece, "cols", swap)
    w_row = lax.all_to_all(
        jnp.broadcast_to(piece[None], (16, 128, OBS)),
        "cols",
        0,
        0,
        axis_index_groups=planes,
        tiled=True,
    ).reshape(8 * LON, OBS)

    gram = jnp.dot(g_row, w_row, precision=HI)
    gram = gram + lax.ppermute(gram, "rows", [(i, i ^ 1) for i in range(rows_n)])
    gram = gram + lax.ppermute(gram, "rows", [(i, i ^ 2) for i in range(rows_n)])
    gram = gram + lax.ppermute(gram, "rows", [(i, i ^ 4) for i in range(rows_n)])
    innovation_cov = gram + jnp.diag(obs_variance)

    w_below = lax.ppermute(w_row[6 * LON :], "rows", up)
    w_above = lax.ppermute(w_row[: 2 * LON], "rows", down)
    (v_row,) = row_step([(w_below, 0, 2), (w_row, 0, 8), (w_above, 0, 2)], down_coef, 0, (8,))

    v_col = lax.dynamic_slice_in_dim(v_row, (c % 4) * 2 * LON, 2 * LON, 0)
    pair, hop1, hop2, hop3 = [], [], [], []
    for col in range(cols_n):
        home = col // 4
        pair.append((home * cols_n + col, (home ^ 1) * cols_n + col))
        for core in range(2):
            z = home // 2
            src = (2 * z + core) * cols_n + col
            for hop, d in ((hop1, 1), (hop2, 2), (hop3, 3)):
                hop.append((src, (2 * ((z + d) % 4) + core) * cols_n + col))
    v_col = jnp.where(r == c // 4, v_col, 0.0)
    v_col = v_col + lax.ppermute(v_col, ("rows", "cols"), pair)
    mine = jnp.where(r // 2 == c // 8, v_col, 0.0)
    v_col = mine
    for hop in (hop1, hop2, hop3):
        v_col = v_col + lax.ppermute(mine, ("rows", "cols"), hop)

    field = prior_concentration.reshape(-1, LON)
    for _ in range(2):
        ext = jnp.pad(field, ((1, 1), (0, 0)))
        field = (
            coefs[0] * field
            + coefs[1] * jnp.roll(field, 1, axis=1)
            + coefs[2] * jnp.roll(field, -1, axis=1)
            + coefs[3] * ext[:-2]
            + coefs[4] * ext[2:]
        )
    flat = sensor_cell_position.reshape(-1)
    lat_hot = (flat[:, None] // LON == jnp.arange(field.shape[0])[None, :]).astype(jnp.float32)
    lines = jnp.dot(lat_hot, field, precision=HI)
    lon_hot = flat[:, None] % LON == jnp.arange(LON)[None, :]
    picked = jnp.sum(jnp.where(lon_hot, lines, 0.0), axis=1).reshape(sensor_cell_position.shape)
    innovation = measurement_readings - jnp.sum(sensor_cell_share * picked, axis=1)

    right_sides = jnp.concatenate(
        [v_col.T, jnp.pad(innovation[:, None], ((0, 0), (0, 127)))], axis=1
    )
    solved = cholesky_solve(innovation_cov, right_sides)
    right = solved[:, : 2 * LON]
    mean_band = lax.dynamic_slice_in_dim(field, 8 * r, 8, 0).reshape(-1)
    corrected = mean_band + jnp.dot(v_row, solved[:, 2 * LON], precision=HI)

    low = row_step([(from_below, 0, 2), (covariance, 0, 4)], down_coef, 0, (2,))
    high = row_step([(covariance, 4, 4), (from_above, 0, 2)], down_coef, 6, (1, 1))
    chunks = [(2, inner[0]), (4, inner[1]), (0, low[0]), (6, high[0]), (7, high[1])]
    flag = (c % 2)[None]
    out = None
    for first_lat, own in chunks:
        swapped = lax.ppermute(own, "cols", swap)
        passed = lax.ppermute(swapped, "cols", onward)
        out = column_step(flag, own, swapped, passed, across_coef, v_row, right, first_lat, out)
    return (out, corrected)


def solution(mesh):
    return jax.shard_map(
        shards,
        mesh=mesh,
        in_specs=(P("rows", "cols"), P(), P(), P(), P(), P(), P(), P(), P()),
        out_specs=(P("rows", "cols"), P("rows")),
        check_vma=False,
    )
```

```python
import functools

import jax
import jax.numpy as jnp
from jax import lax
from jax.experimental import pallas as pl
from jax.experimental.pallas import tpu as pltpu
from jax.sharding import PartitionSpec as P

HI = lax.Precision.HIGHEST
LON = 256
OBS = 128
SMALL = pl.CostEstimate(flops=1, bytes_accessed=1, transcendentals=0)


def after(value, *others):
    return lax.optimization_barrier((value, *others))[0]


def coefficients(east_wind, north_wind, diffusivity):
    western = jnp.maximum(east_wind, 0.0) + diffusivity
    eastern = jnp.maximum(-east_wind, 0.0) + diffusivity
    southern = jnp.maximum(north_wind, 0.0) + diffusivity
    northern = jnp.maximum(-north_wind, 0.0) + diffusivity
    middle = 1.0 - (western + eastern + southern + northern)
    return (middle, western, eastern, southern, northern)


def row_kernel(groups, n_in, outs, *refs):
    coef = refs[n_in]
    out_refs = refs[n_in + 1 : n_in + 1 + len(outs)]
    wide, mid = refs[n_in + 1 + len(outs) :]

    @pl.when(pl.program_id(0) == 0)
    def _():
        at = 0
        for _, off, n in groups:
            for j in range(n + 2):
                for k in range(5):
                    column = coef[(off + j) * LON : (off + j + 1) * LON, k : k + 1]
                    wide[k, at + j] = jnp.broadcast_to(column, (LON, 128))
            at += n + 2

    def step(j, here, south, north):
        west = pltpu.roll(here, 1, axis=0)
        east = pltpu.roll(here, LON - 1, axis=0)
        return (
            wide[0, j] * here
            + wide[1, j] * west
            + wide[2, j] * east
            + wide[3, j] * south
            + wide[4, j] * north
        )

    places = [(ref, i) for ref, count in zip(out_refs, outs) for i in range(count)]
    at = 0
    for sources, _, n in groups:

        def source(i):
            which, lat = sources[i]
            return refs[which][lat * LON : (lat + 1) * LON, :]

        for j in range(n + 2):
            mid[j] = step(at + j, source(j + 1), source(j), source(j + 2))
        for j in range(1, n + 1):
            ref, i = places.pop(0)
            ref[i * LON : (i + 1) * LON, :] = step(at + j, mid[j], mid[j - 1], mid[j + 1])
        at += n + 2


def row_steps(arrays, coef, groups, outs):
    cols = arrays[0].shape[1]
    total = sum(n + 2 for _, _, n in groups)
    return pl.pallas_call(
        functools.partial(row_kernel, groups, len(arrays), outs),
        grid=(cols // 128,),
        in_specs=[pl.BlockSpec((a.shape[0], 128), lambda i: (0, i)) for a in arrays]
        + [pl.BlockSpec(coef.shape, lambda i: (0, 0))],
        out_specs=[pl.BlockSpec((count * LON, 128), lambda i: (0, i)) for count in outs],
        out_shape=[jax.ShapeDtypeStruct((count * LON, cols), jnp.float32) for count in outs],
        scratch_shapes=[
            pltpu.VMEM((5, total, LON, 128), jnp.float32),
            pltpu.VMEM((max(n for _, _, n in groups) + 2, LON, 128), jnp.float32),
        ],
        compiler_params=pltpu.CompilerParams(vmem_limit_bytes=60 << 20),
        cost_estimate=SMALL,
        name="row_step",
    )(*arrays, coef)


def inner_step(own, coef):
    return row_steps([own], coef, [([(0, i) for i in range(8)], 2, 4)], (2, 2))


def edge_step(below, own, above, coef):
    first = [(0, 0), (0, 1)] + [(1, i) for i in range(4)]
    second = [(1, i) for i in range(4, 8)] + [(2, 0), (2, 1)]
    return row_steps([below, own, above], coef, [(first, 0, 2), (second, 6, 2)], (2, 2))


TILE = 16


def column_kernel(mode, block, flag, *refs):
    blocks, coef, out, wide = refs[:-3], refs[-3], refs[-2], refs[-1]

    @pl.when(pl.program_id(0) == 0)
    def _():
        for i in range(20):
            wide[i] = jnp.broadcast_to(coef[i : i + 1, :], (8, LON))

    low_bit = flag[0]
    zero = jnp.zeros((TILE, LON), jnp.float32)

    def times(i, x):
        return x if x is zero else jnp.concatenate([wide[i]] * (TILE // 8), 0) * x

    def step(j, here, south, north):
        if here is zero:
            terms = []
        else:
            terms = [
                times(5 * j, here),
                times(5 * j + 1, pltpu.roll(here, 1, axis=1)),
                times(5 * j + 2, pltpu.roll(here, LON - 1, axis=1)),
            ]
        terms += [times(5 * j + 3, south)] if south is not zero else []
        terms += [times(5 * j + 4, north)] if north is not zero else []
        return functools.reduce(lambda x, y: x + y, terms)

    def tile(t, carry):
        at = pl.ds(pl.multiple_of(t * TILE, TILE), TILE)
        f = [zero] * 6
        if mode != "others":
            f[2], f[3] = blocks[0][at, :LON], blocks[0][at, LON:]
        if mode != "own":
            near, far = blocks[-2][at, :], blocks[-1][at, :]
            below = jnp.where(low_bit == 0, far, near)
            above = jnp.where(low_bit == 0, near, far)
            f[0], f[1], f[4], f[5] = below[:, :LON], below[:, LON:], above[:, :LON], above[:, LON:]
        g = [step(j, f[j + 1], f[j], f[j + 2]) for j in range(4)]
        out[at, :LON] = step(1, g[1], g[0], g[2])
        out[at, LON:] = step(2, g[2], g[1], g[3])
        return carry

    lax.fori_loop(0, block // TILE, tile, 0, unroll=4)


def column_step(mode, flag, blocks, coef):
    rows, block = blocks[0].shape[0], 128
    spec = pl.BlockSpec((block, 2 * LON), lambda i: (i, 0))
    return pl.pallas_call(
        functools.partial(column_kernel, mode, block),
        grid=(rows // block,),
        in_specs=[pl.BlockSpec(memory_space=pltpu.SMEM)]
        + [spec] * len(blocks)
        + [pl.BlockSpec(coef.shape, lambda i: (0, 0))],
        out_specs=spec,
        out_shape=jax.ShapeDtypeStruct((rows, 2 * LON), jnp.float32),
        scratch_shapes=[pltpu.VMEM((20, 8, LON), jnp.float32)],
        compiler_params=pltpu.CompilerParams(vmem_limit_bytes=40 << 20),
        cost_estimate=SMALL,
        name="column_step_" + mode,
    )(flag, *blocks, coef)


def correct_kernel(n, *refs):
    left, right, out = refs[n], refs[n + 1], refs[-1]
    forecast = refs[0][...] if n == 1 else refs[0][...] + refs[1][...]
    out[...] = forecast - jnp.dot(
        left[...], right[...], precision=HI, preferred_element_type=jnp.float32
    )


def correct(terms, left, right, first_lat, into):
    rows, n = terms[0].shape[0], len(terms)
    aliased = [] if into is None else [into]
    return pl.pallas_call(
        functools.partial(correct_kernel, n),
        grid=(rows // LON,),
        in_specs=[pl.BlockSpec((LON, 2 * LON), lambda i: (i, 0))] * n
        + [
            pl.BlockSpec((LON, OBS), lambda i: (first_lat + i, 0)),
            pl.BlockSpec(right.shape, lambda i: (0, 0)),
        ]
        + [pl.BlockSpec(memory_space=pl.ANY)] * len(aliased),
        out_specs=pl.BlockSpec((LON, 2 * LON), lambda i: (first_lat + i, 0)),
        out_shape=jax.ShapeDtypeStruct((8 * LON, 2 * LON), jnp.float32),
        input_output_aliases={n + 2: 0} if aliased else {},
        compiler_params=pltpu.CompilerParams(vmem_limit_bytes=40 << 20),
        cost_estimate=SMALL,
        name="correct",
    )(*terms, left, right, *aliased)


def adjoint_kernel(n, start, position, share, coef, out, first, second):
    lane = lax.broadcasted_iota(jnp.int32, (OBS, LON), 1)
    for i in range(n + 4):
        base = start[0] + i * LON
        total = jnp.zeros((OBS, LON), jnp.float32)
        for f in range(position.shape[1]):
            hit = (position[:, f : f + 1] - base) == lane
            total = total + jnp.where(hit, share[:, f : f + 1], 0.0)
        first[i] = total

    def adjoint(field, i):
        def c(k, j):
            return coef[k * (n + 4) + j : k * (n + 4) + j + 1, :]

        here = field[i]
        return (
            c(0, i) * here
            + pltpu.roll(c(1, i) * here, LON - 1, axis=1)
            + pltpu.roll(c(2, i) * here, 1, axis=1)
            + c(3, i + 1) * field[i + 1]
            + c(4, i - 1) * field[i - 1]
        )

    for i in range(1, n + 3):
        second[i] = adjoint(first, i)
    for i in range(2, n + 2):
        out[:, (i - 2) * LON : (i - 1) * LON] = adjoint(second, i)


def adjoint_footprints(start, position, share, coef, n):
    vmem = pl.BlockSpec(memory_space=pltpu.VMEM)
    return pl.pallas_call(
        functools.partial(adjoint_kernel, n),
        in_specs=[pl.BlockSpec(memory_space=pltpu.SMEM), vmem, vmem, vmem],
        out_specs=vmem,
        out_shape=jax.ShapeDtypeStruct((OBS, n * LON), jnp.float32),
        scratch_shapes=[pltpu.VMEM((n + 4, OBS, LON), jnp.float32)] * 2,
        compiler_params=pltpu.CompilerParams(vmem_limit_bytes=40 << 20),
        cost_estimate=SMALL,
        name="adjoint_footprints",
    )(start, position, share, coef)


def footprints_kernel(lats, start, position, share, out):
    lane = lax.broadcasted_iota(jnp.int32, (OBS, LON), 1)
    for i in range(lats):
        base = start[0] + i * LON
        total = jnp.zeros((OBS, LON), jnp.float32)
        for f in range(position.shape[1]):
            hit = (position[:, f : f + 1] - base) == lane
            total = total + jnp.where(hit, share[:, f : f + 1], 0.0)
        out[:, i * LON : (i + 1) * LON] = total


def footprints(start, position, share, lats):
    vmem = pl.BlockSpec(memory_space=pltpu.VMEM)
    return pl.pallas_call(
        functools.partial(footprints_kernel, lats),
        in_specs=[pl.BlockSpec(memory_space=pltpu.SMEM), vmem, vmem],
        out_specs=vmem,
        out_shape=jax.ShapeDtypeStruct((OBS, lats * LON), jnp.float32),
        compiler_params=pltpu.CompilerParams(vmem_limit_bytes=40 << 20),
        cost_estimate=SMALL,
        name="footprints",
    )(start, position, share)


def dot_rows(a, b):
    return lax.dot_general(
        a, b, (((1,), (1,)), ((), ())), precision=HI, preferred_element_type=jnp.float32
    )


def project_kernel(*refs):
    blocks, g, v_out = refs[:-2], refs[-2], refs[-1]
    at = 0
    for ref in blocks:
        for i in range(0, ref.shape[0], LON):
            v_out[at : at + LON, :] = dot_rows(ref[i : i + LON, :], g[...])
            at += LON


def project(blocks, g):
    vmem = pl.BlockSpec(memory_space=pltpu.VMEM)
    rows = sum(a.shape[0] for a in blocks)
    return pl.pallas_call(
        project_kernel,
        in_specs=[vmem] * (len(blocks) + 1),
        out_specs=vmem,
        out_shape=jax.ShapeDtypeStruct((rows, OBS), jnp.float32),
        compiler_params=pltpu.CompilerParams(vmem_limit_bytes=40 << 20),
        cost_estimate=SMALL,
        name="project",
    )(*blocks, g)


def inverse_kernel(gram, variance, out):
    row = lax.broadcasted_iota(jnp.int32, (OBS, OBS), 0)
    lane = lax.broadcasted_iota(jnp.int32, (OBS, OBS), 1)
    a = gram[...] + jnp.where(row == lane, variance[...], 0.0)
    at = lax.broadcasted_iota(jnp.int32, (1, OBS), 1)
    for k in range(OBS):
        column = jnp.broadcast_to(a[:, k : k + 1], (OBS, OBS))
        pivot = 1.0 / column[k : k + 1, :]
        line = jnp.where(at == k, 1.0, a[k : k + 1, :]) * pivot
        a = jnp.where(lane == k, 0.0, a) - column * line
        a = jnp.where(row == k, line, a)
    out[...] = a


def inverse(gram, variance):
    vmem = pl.BlockSpec(memory_space=pltpu.VMEM)
    return pl.pallas_call(
        inverse_kernel,
        in_specs=[vmem, vmem],
        out_specs=vmem,
        out_shape=jax.ShapeDtypeStruct((OBS, OBS), jnp.float32),
        cost_estimate=SMALL,
        name="inverse",
    )(gram, variance)


def shards(
    covariance,
    prior_concentration,
    east_wind,
    north_wind,
    diffusivity,
    sensor_cell_position,
    sensor_cell_share,
    measurement_readings,
    obs_variance,
):
    rows_n, cols_n = lax.axis_size("rows"), lax.axis_size("cols")
    r, c = lax.axis_index("rows"), lax.axis_index("cols")
    up = [(i, i + 1) for i in range(rows_n - 1)]
    down = [(j, i) for i, j in up]
    swap = [(i, i ^ 1) for i in range(cols_n)]
    onward = [(i, i + 2) for i in range(0, cols_n - 2, 2)]
    onward += [(i, i - 2) for i in range(3, cols_n, 2)]
    planes = [[2 * i + k for i in range(cols_n // 2)] for k in range(2)]

    from_below = lax.ppermute(covariance[6 * LON :], "rows", up)
    from_above = lax.ppermute(covariance[: 2 * LON], "rows", down)

    coefs = coefficients(east_wind, north_wind, diffusivity)
    padded = jnp.pad(jnp.stack(coefs), ((0, 0), (2, 2), (0, 0)))
    row_band = lax.dynamic_slice_in_dim(padded, 8 * r, 12, 1)
    col_band = lax.dynamic_slice_in_dim(padded, 2 * c, 6, 1)
    down_coef = jnp.pad(row_band[:, 1:11].reshape(5, 10 * LON).T, ((0, 0), (0, 3)))
    across_coef = jnp.pad(col_band[:, 1:5].transpose(1, 0, 2).reshape(20, LON), ((0, 4), (0, 0)))

    inner = inner_step(covariance, down_coef)

    flag = (c % 2)[None]

    back = [(i, i + 2) for i in range(1, cols_n - 2, 2)]
    back += [(i, i - 2) for i in range(2, cols_n, 2)]
    other_band = lax.dynamic_slice_in_dim(padded, 2 * (c ^ 1), 6, 1)
    other_coef = jnp.pad(
        other_band[:, 1:5].transpose(1, 0, 2).reshape(20, LON), ((0, 4), (0, 0))
    )
    a1, b1 = inner
    got_a1 = lax.ppermute(a1, "cols", swap)
    raw_b1 = lax.ppermute(b1, "cols", back)

    g_col = adjoint_footprints(
        ((2 * c - 2) * LON)[None],
        sensor_cell_position,
        sensor_cell_share,
        col_band.reshape(30, LON),
        2,
    )
    v_inner = project([a1, b1], g_col)

    a2, b2 = edge_step(from_below, covariance, from_above, down_coef)
    got_a2 = lax.ppermute(a2, "cols", swap)
    raw_b2 = lax.ppermute(b2, "cols", back)
    v_outer = project([a2, b2], g_col)
    v_part = jnp.concatenate([v_outer[: 2 * LON], v_inner, v_outer[2 * LON :]])

    field = prior_concentration.reshape(-1, LON)
    for _ in range(2):
        ext = jnp.pad(field, ((1, 1), (0, 0)))
        field = (
            coefs[0] * field
            + coefs[1] * jnp.roll(field, 1, axis=1)
            + coefs[2] * jnp.roll(field, -1, axis=1)
            + coefs[3] * ext[:-2]
            + coefs[4] * ext[2:]
        )
    flat = sensor_cell_position.reshape(-1)
    lat_hot = (flat[:, None] // LON == jnp.arange(field.shape[0])[None, :]).astype(jnp.float32)
    lines = jnp.dot(lat_hot, field, precision=HI)
    lon_hot = flat[:, None] % LON == jnp.arange(LON)[None, :]
    picked = jnp.sum(jnp.where(lon_hot, lines, 0.0), axis=1).reshape(sensor_cell_position.shape)
    innovation = measurement_readings - jnp.sum(sensor_cell_share * picked, axis=1)

    arrived = lax.all_to_all(
        v_part.reshape(16, 128, OBS), "cols", 0, 0, axis_index_groups=planes, tiled=True
    )
    far_a1 = lax.ppermute(got_a1, "cols", onward)
    part_b1 = column_step("others", 1 - flag, [b1, raw_b1], other_coef)
    part_b2 = column_step("others", 1 - flag, [b2, raw_b2], other_coef)
    piece = after(arrived, part_b1, got_a1).sum(axis=0)
    other = lax.ppermute(piece, "cols", swap)
    sum_b1 = lax.ppermute(after(part_b1, piece), "cols", swap)
    h_row = footprints((8 * r * LON)[None], sensor_cell_position, sensor_cell_share, 8)
    whole = lax.all_to_all(
        jnp.broadcast_to(after(piece + other, got_a2)[None], (16, 128, OBS)),
        "cols",
        0,
        0,
        axis_index_groups=planes,
        tiled=True,
    )
    v_row = after(whole, h_row, part_b2, sum_b1, far_a1, innovation).reshape(8 * LON, OBS)
    far_a2 = lax.ppermute(after(got_a2, v_row), "cols", onward)

    gram = jnp.dot(h_row, v_row, precision=HI)
    v_col = lax.dynamic_slice_in_dim(v_row, (c % 4) * 2 * LON, 2 * LON, 0)
    v_col = jnp.where(r == c // 4, v_col, 0.0)
    both = jnp.concatenate([gram, v_col])
    both = both + lax.ppermute(both, "rows", [(i, i ^ 1) for i in range(rows_n)])
    gram, v_col = both[:OBS], both[OBS:]
    gram = gram + lax.ppermute(gram, "rows", [(i, i ^ 2) for i in range(rows_n)])
    gram = gram + lax.ppermute(gram, "rows", [(i, i ^ 4) for i in range(rows_n)])
    mine = jnp.where(r // 2 == c // 8, v_col, 0.0)
    v_col = mine
    for d in (1, 2, 3):
        hop = []
        for col in range(cols_n):
            z = col // 8
            for core in range(2):
                src, dst = 2 * z + core, 2 * ((z + d) % 4) + core
                hop.append((src * cols_n + col, dst * cols_n + col))
        v_col = v_col + lax.ppermute(mine, ("rows", "cols"), hop)
    own_b1 = column_step("own", flag, [after(b1, v_row)], across_coef)
    own_b2 = column_step("own", flag, [after(b2, v_row)], across_coef)
    f_a1 = column_step("all", flag, [after(a1, v_row), got_a1, far_a1], across_coef)
    gram, v_col, own_b1, own_b2, f_a1, _ = lax.optimization_barrier(
        (gram, v_col, own_b1, own_b2, f_a1, far_a2)
    )
    sum_b2 = lax.ppermute(after(part_b2, gram), "cols", swap)

    weights = inverse(gram, obs_variance[None])
    f_a2 = column_step("all", flag, [a2, got_a2, far_a2], across_coef)
    right = dot_rows(weights, v_col)
    solved = jnp.sum(weights * innovation[None], axis=1)
    mean_band = lax.dynamic_slice_in_dim(field, 8 * r, 8, 0).reshape(-1)
    corrected = mean_band + jnp.sum(v_row * solved[None], axis=1)

    out = None
    for first_lat, terms in (
        (4, [own_b1, sum_b1]),
        (2, [f_a1]),
        (6, [own_b2, sum_b2]),
        (0, [f_a2]),
    ):
        out = correct(terms, v_row, right, first_lat, out)
    return (out, corrected)


def solution(mesh):
    return jax.shard_map(
        shards,
        mesh=mesh,
        in_specs=(P("rows", "cols"), P(), P(), P(), P(), P(), P(), P(), P()),
        out_specs=(P("rows", "cols"), P("rows")),
        check_vma=False,
    )
```

```python
import functools

import jax
import jax.numpy as jnp
from jax import lax
from jax.experimental import pallas as pl
from jax.experimental.pallas import tpu as pltpu
from jax.sharding import PartitionSpec as P

HI = lax.Precision.HIGHEST
LON = 256
OBS = 128
SMALL = pl.CostEstimate(flops=1, bytes_accessed=1, transcendentals=0)


def after(value, *others):
    return lax.optimization_barrier((value, *others))[0]


def coefficients(east_wind, north_wind, diffusivity):
    western = jnp.maximum(east_wind, 0.0) + diffusivity
    eastern = jnp.maximum(-east_wind, 0.0) + diffusivity
    southern = jnp.maximum(north_wind, 0.0) + diffusivity
    northern = jnp.maximum(-north_wind, 0.0) + diffusivity
    middle = 1.0 - (western + eastern + southern + northern)
    return (middle, western, eastern, southern, northern)


def row_kernel(groups, n_in, outs, *refs):
    coef = refs[n_in]
    out_refs = refs[n_in + 1 : n_in + 1 + len(outs)]
    wide, mid = refs[n_in + 1 + len(outs) :]

    @pl.when(pl.program_id(0) == 0)
    def _():
        at = 0
        for _, off, n in groups:
            for j in range(n + 2):
                for k in range(5):
                    column = coef[(off + j) * LON : (off + j + 1) * LON, k : k + 1]
                    wide[k, at + j] = jnp.broadcast_to(column, (LON, 128))
            at += n + 2

    def step(j, here, south, north):
        west = pltpu.roll(here, 1, axis=0)
        east = pltpu.roll(here, LON - 1, axis=0)
        return (
            wide[0, j] * here
            + wide[1, j] * west
            + wide[2, j] * east
            + wide[3, j] * south
            + wide[4, j] * north
        )

    places = [(ref, i) for ref, count in zip(out_refs, outs) for i in range(count)]
    at = 0
    for sources, _, n in groups:

        def source(i):
            which, lat = sources[i]
            return refs[which][lat * LON : (lat + 1) * LON, :]

        for j in range(n + 2):
            mid[j] = step(at + j, source(j + 1), source(j), source(j + 2))
        for j in range(1, n + 1):
            ref, i = places.pop(0)
            ref[i * LON : (i + 1) * LON, :] = step(at + j, mid[j], mid[j - 1], mid[j + 1])
        at += n + 2


def row_steps(arrays, coef, groups, outs):
    cols = arrays[0].shape[1]
    total = sum(n + 2 for _, _, n in groups)
    return pl.pallas_call(
        functools.partial(row_kernel, groups, len(arrays), outs),
        grid=(cols // 128,),
        in_specs=[pl.BlockSpec((a.shape[0], 128), lambda i: (0, i)) for a in arrays]
        + [pl.BlockSpec(coef.shape, lambda i: (0, 0))],
        out_specs=[pl.BlockSpec((count * LON, 128), lambda i: (0, i)) for count in outs],
        out_shape=[jax.ShapeDtypeStruct((count * LON, cols), jnp.float32) for count in outs],
        scratch_shapes=[
            pltpu.VMEM((5, total, LON, 128), jnp.float32),
            pltpu.VMEM((max(n for _, _, n in groups) + 2, LON, 128), jnp.float32),
        ],
        compiler_params=pltpu.CompilerParams(vmem_limit_bytes=16 << 20),
        cost_estimate=SMALL,
        name="row_step",
    )(*arrays, coef)


def inner_step(own, coef):
    return row_steps([own], coef, [([(0, i) for i in range(8)], 2, 4)], (2, 2))


def edge_step(below, own, above, coef):
    first = [(0, 0), (0, 1)] + [(1, i) for i in range(4)]
    second = [(1, i) for i in range(4, 8)] + [(2, 0), (2, 1)]
    return row_steps([below, own, above], coef, [(first, 0, 2), (second, 6, 2)], (2, 2))


TILE = 16


def column_kernel(mode, block, flag, *refs):
    blocks, coef, out, wide = refs[:-3], refs[-3], refs[-2], refs[-1]

    @pl.when(pl.program_id(0) == 0)
    def _():
        for i in range(20):
            wide[i] = jnp.broadcast_to(coef[i : i + 1, :], (8, LON))

    low_bit = flag[0]
    zero = jnp.zeros((TILE, LON), jnp.float32)

    def times(i, x):
        return x if x is zero else jnp.concatenate([wide[i]] * (TILE // 8), 0) * x

    def step(j, here, south, north):
        if here is zero:
            terms = []
        else:
            terms = [
                times(5 * j, here),
                times(5 * j + 1, pltpu.roll(here, 1, axis=1)),
                times(5 * j + 2, pltpu.roll(here, LON - 1, axis=1)),
            ]
        terms += [times(5 * j + 3, south)] if south is not zero else []
        terms += [times(5 * j + 4, north)] if north is not zero else []
        return functools.reduce(lambda x, y: x + y, terms)

    def tile(t, carry):
        at = pl.ds(pl.multiple_of(t * TILE, TILE), TILE)
        f = [zero] * 6
        if mode != "others":
            f[2], f[3] = blocks[0][at, :LON], blocks[0][at, LON:]
        if mode != "own":
            near, far = blocks[-2][at, :], blocks[-1][at, :]
            below = jnp.where(low_bit == 0, far, near)
            above = jnp.where(low_bit == 0, near, far)
            f[0], f[1], f[4], f[5] = below[:, :LON], below[:, LON:], above[:, :LON], above[:, LON:]
        g = [step(j, f[j + 1], f[j], f[j + 2]) for j in range(4)]
        out[at, :LON] = step(1, g[1], g[0], g[2])
        out[at, LON:] = step(2, g[2], g[1], g[3])
        return carry

    lax.fori_loop(0, block // TILE, tile, 0, unroll=4)


def column_step(mode, flag, blocks, coef):
    rows, block = blocks[0].shape[0], 128
    spec = pl.BlockSpec((block, 2 * LON), lambda i: (i, 0))
    return pl.pallas_call(
        functools.partial(column_kernel, mode, block),
        grid=(rows // block,),
        in_specs=[pl.BlockSpec(memory_space=pltpu.SMEM)]
        + [spec] * len(blocks)
        + [pl.BlockSpec(coef.shape, lambda i: (0, 0))],
        out_specs=spec,
        out_shape=jax.ShapeDtypeStruct((rows, 2 * LON), jnp.float32),
        scratch_shapes=[pltpu.VMEM((20, 8, LON), jnp.float32)],
        compiler_params=pltpu.CompilerParams(vmem_limit_bytes=16 << 20),
        cost_estimate=SMALL,
        name="column_step_" + mode,
    )(flag, *blocks, coef)


def correct_kernel(n, *refs):
    left, right, out = refs[n], refs[n + 1], refs[-1]
    forecast = refs[0][...] if n == 1 else refs[0][...] + refs[1][...]
    out[...] = forecast - jnp.dot(
        left[...], right[...], precision=HI, preferred_element_type=jnp.float32
    )


def correct(terms, left, right, first_lat, into):
    rows, n = terms[0].shape[0], len(terms)
    aliased = [] if into is None else [into]
    return pl.pallas_call(
        functools.partial(correct_kernel, n),
        grid=(rows // LON,),
        in_specs=[pl.BlockSpec((LON, 2 * LON), lambda i: (i, 0))] * n
        + [
            pl.BlockSpec((LON, OBS), lambda i: (first_lat + i, 0)),
            pl.BlockSpec(right.shape, lambda i: (0, 0)),
        ]
        + [pl.BlockSpec(memory_space=pl.ANY)] * len(aliased),
        out_specs=pl.BlockSpec((LON, 2 * LON), lambda i: (first_lat + i, 0)),
        out_shape=jax.ShapeDtypeStruct((8 * LON, 2 * LON), jnp.float32),
        input_output_aliases={n + 2: 0} if aliased else {},
        compiler_params=pltpu.CompilerParams(vmem_limit_bytes=16 << 20),
        cost_estimate=SMALL,
        name="correct",
    )(*terms, left, right, *aliased)


def adjoint_kernel(n, start, position, share, coef, out, first, second):
    lane = lax.broadcasted_iota(jnp.int32, (OBS, LON), 1)
    for i in range(n + 4):
        base = start[0] + i * LON
        total = jnp.zeros((OBS, LON), jnp.float32)
        for f in range(position.shape[1]):
            hit = (position[:, f : f + 1] - base) == lane
            total = total + jnp.where(hit, share[:, f : f + 1], 0.0)
        first[i] = total

    def adjoint(field, i):
        def c(k, j):
            return coef[k * (n + 4) + j : k * (n + 4) + j + 1, :]

        here = field[i]
        return (
            c(0, i) * here
            + pltpu.roll(c(1, i) * here, LON - 1, axis=1)
            + pltpu.roll(c(2, i) * here, 1, axis=1)
            + c(3, i + 1) * field[i + 1]
            + c(4, i - 1) * field[i - 1]
        )

    for i in range(1, n + 3):
        second[i] = adjoint(first, i)
    for i in range(2, n + 2):
        out[:, (i - 2) * LON : (i - 1) * LON] = adjoint(second, i)


def adjoint_footprints(start, position, share, coef, n):
    vmem = pl.BlockSpec(memory_space=pltpu.VMEM)
    return pl.pallas_call(
        functools.partial(adjoint_kernel, n),
        in_specs=[pl.BlockSpec(memory_space=pltpu.SMEM), vmem, vmem, vmem],
        out_specs=vmem,
        out_shape=jax.ShapeDtypeStruct((OBS, n * LON), jnp.float32),
        scratch_shapes=[pltpu.VMEM((n + 4, OBS, LON), jnp.float32)] * 2,
        compiler_params=pltpu.CompilerParams(vmem_limit_bytes=16 << 20),
        cost_estimate=SMALL,
        name="adjoint_footprints",
    )(start, position, share, coef)


def footprints_kernel(lats, start, position, share, out):
    lane = lax.broadcasted_iota(jnp.int32, (OBS, LON), 1)
    for i in range(lats):
        base = start[0] + i * LON
        total = jnp.zeros((OBS, LON), jnp.float32)
        for f in range(position.shape[1]):
            hit = (position[:, f : f + 1] - base) == lane
            total = total + jnp.where(hit, share[:, f : f + 1], 0.0)
        out[:, i * LON : (i + 1) * LON] = total


def footprints(start, position, share, lats):
    vmem = pl.BlockSpec(memory_space=pltpu.VMEM)
    return pl.pallas_call(
        functools.partial(footprints_kernel, lats),
        in_specs=[pl.BlockSpec(memory_space=pltpu.SMEM), vmem, vmem],
        out_specs=vmem,
        out_shape=jax.ShapeDtypeStruct((OBS, lats * LON), jnp.float32),
        compiler_params=pltpu.CompilerParams(vmem_limit_bytes=16 << 20),
        cost_estimate=SMALL,
        name="footprints",
    )(start, position, share)


def dot_rows(a, b):
    return lax.dot_general(
        a, b, (((1,), (1,)), ((), ())), precision=HI, preferred_element_type=jnp.float32
    )


def project_kernel(*refs):
    blocks, g, v_out = refs[:-2], refs[-2], refs[-1]
    at = 0
    for ref in blocks:
        for i in range(0, ref.shape[0], LON):
            v_out[at : at + LON, :] = dot_rows(ref[i : i + LON, :], g[...])
            at += LON


def project(blocks, g):
    vmem = pl.BlockSpec(memory_space=pltpu.VMEM)
    rows = sum(a.shape[0] for a in blocks)
    return pl.pallas_call(
        project_kernel,
        in_specs=[vmem] * (len(blocks) + 1),
        out_specs=vmem,
        out_shape=jax.ShapeDtypeStruct((rows, OBS), jnp.float32),
        compiler_params=pltpu.CompilerParams(vmem_limit_bytes=16 << 20),
        cost_estimate=SMALL,
        name="project",
    )(*blocks, g)


def inverse_kernel(gram, variance, out):
    row = lax.broadcasted_iota(jnp.int32, (OBS, OBS), 0)
    lane = lax.broadcasted_iota(jnp.int32, (OBS, OBS), 1)
    a = gram[...] + jnp.where(row == lane, variance[...], 0.0)
    at = lax.broadcasted_iota(jnp.int32, (1, OBS), 1)
    for k in range(OBS):
        column = jnp.broadcast_to(a[:, k : k + 1], (OBS, OBS))
        pivot = 1.0 / column[k : k + 1, :]
        line = jnp.where(at == k, 1.0, a[k : k + 1, :]) * pivot
        a = jnp.where(lane == k, 0.0, a) - column * line
        a = jnp.where(row == k, line, a)
    out[...] = a


def inverse(gram, variance):
    vmem = pl.BlockSpec(memory_space=pltpu.VMEM)
    return pl.pallas_call(
        inverse_kernel,
        in_specs=[vmem, vmem],
        out_specs=vmem,
        out_shape=jax.ShapeDtypeStruct((OBS, OBS), jnp.float32),
        cost_estimate=SMALL,
        name="inverse",
    )(gram, variance)


def shards(
    covariance,
    prior_concentration,
    east_wind,
    north_wind,
    diffusivity,
    sensor_cell_position,
    sensor_cell_share,
    measurement_readings,
    obs_variance,
):
    rows_n, cols_n = lax.axis_size("rows"), lax.axis_size("cols")
    r, c = lax.axis_index("rows"), lax.axis_index("cols")
    up = [(i, i + 1) for i in range(rows_n - 1)]
    down = [(j, i) for i, j in up]
    swap = [(i, i ^ 1) for i in range(cols_n)]
    onward = [(i, i + 2) for i in range(0, cols_n - 2, 2)]
    onward += [(i, i - 2) for i in range(3, cols_n, 2)]
    planes = [[2 * i + k for i in range(cols_n // 2)] for k in range(2)]

    from_below = lax.ppermute(covariance[6 * LON :], "rows", up)
    from_above = lax.ppermute(covariance[: 2 * LON], "rows", down)

    coefs = coefficients(east_wind, north_wind, diffusivity)
    padded = jnp.pad(jnp.stack(coefs), ((0, 0), (2, 2), (0, 0)))
    row_band = lax.dynamic_slice_in_dim(padded, 8 * r, 12, 1)
    col_band = lax.dynamic_slice_in_dim(padded, 2 * c, 6, 1)
    down_coef = jnp.pad(row_band[:, 1:11].reshape(5, 10 * LON).T, ((0, 0), (0, 3)))
    across_coef = jnp.pad(col_band[:, 1:5].transpose(1, 0, 2).reshape(20, LON), ((0, 4), (0, 0)))

    inner = inner_step(covariance, down_coef)

    flag = (c % 2)[None]

    back = [(i, i + 2) for i in range(1, cols_n - 2, 2)]
    back += [(i, i - 2) for i in range(2, cols_n, 2)]
    other_band = lax.dynamic_slice_in_dim(padded, 2 * (c ^ 1), 6, 1)
    other_coef = jnp.pad(
        other_band[:, 1:5].transpose(1, 0, 2).reshape(20, LON), ((0, 4), (0, 0))
    )
    a1, b1 = inner
    got_a1 = lax.ppermute(a1, "cols", swap)
    raw_b1 = lax.ppermute(b1, "cols", back)

    g_col = adjoint_footprints(
        ((2 * c - 2) * LON)[None],
        sensor_cell_position,
        sensor_cell_share,
        col_band.reshape(30, LON),
        2,
    )
    v_inner = project([a1, b1], g_col)

    a2, b2 = edge_step(from_below, covariance, from_above, down_coef)
    got_a2 = lax.ppermute(a2, "cols", swap)
    raw_b2 = lax.ppermute(b2, "cols", back)
    v_outer = project([a2, b2], g_col)
    v_part = jnp.concatenate([v_outer[: 2 * LON], v_inner, v_outer[2 * LON :]])

    field = prior_concentration.reshape(-1, LON)
    for _ in range(2):
        ext = jnp.pad(field, ((1, 1), (0, 0)))
        field = (
            coefs[0] * field
            + coefs[1] * jnp.roll(field, 1, axis=1)
            + coefs[2] * jnp.roll(field, -1, axis=1)
            + coefs[3] * ext[:-2]
            + coefs[4] * ext[2:]
        )
    flat = sensor_cell_position.reshape(-1)
    lat_hot = (flat[:, None] // LON == jnp.arange(field.shape[0])[None, :]).astype(jnp.float32)
    lines = jnp.dot(lat_hot, field, precision=HI)
    lon_hot = flat[:, None] % LON == jnp.arange(LON)[None, :]
    picked = jnp.sum(jnp.where(lon_hot, lines, 0.0), axis=1).reshape(sensor_cell_position.shape)
    innovation = measurement_readings - jnp.sum(sensor_cell_share * picked, axis=1)

    arrived = lax.all_to_all(
        v_part.reshape(16, 128, OBS), "cols", 0, 0, axis_index_groups=planes, tiled=True
    )
    far_a1 = lax.ppermute(got_a1, "cols", onward)
    part_b1 = column_step("others", 1 - flag, [b1, raw_b1], other_coef)
    part_b2 = column_step("others", 1 - flag, [b2, raw_b2], other_coef)
    piece = after(arrived, part_b1, got_a1).sum(axis=0)
    other = lax.ppermute(piece, "cols", swap)
    sum_b1 = lax.ppermute(after(part_b1, piece), "cols", swap)
    h_row = footprints((8 * r * LON)[None], sensor_cell_position, sensor_cell_share, 8)
    whole = lax.all_to_all(
        jnp.broadcast_to(after(piece + other, got_a2)[None], (16, 128, OBS)),
        "cols",
        0,
        0,
        axis_index_groups=planes,
        tiled=True,
    )
    v_row = after(whole, h_row, part_b2, sum_b1, far_a1, innovation).reshape(8 * LON, OBS)
    far_a2 = lax.ppermute(after(got_a2, v_row), "cols", onward)

    gram = jnp.dot(h_row, v_row, precision=HI)
    v_col = lax.dynamic_slice_in_dim(v_row, (c % 4) * 2 * LON, 2 * LON, 0)
    v_col = jnp.where(r == c // 4, v_col, 0.0)
    both = jnp.concatenate([gram, v_col])
    both = both + lax.ppermute(both, "rows", [(i, i ^ 1) for i in range(rows_n)])
    gram, v_col = both[:OBS], both[OBS:]
    gram = gram + lax.ppermute(gram, "rows", [(i, i ^ 2) for i in range(rows_n)])
    gram = gram + lax.ppermute(gram, "rows", [(i, i ^ 4) for i in range(rows_n)])
    mine = jnp.where(r // 2 == c // 8, v_col, 0.0)
    v_col = mine
    for d in (1, 2, 3):
        hop = []
        for col in range(cols_n):
            z = col // 8
            for core in range(2):
                src, dst = 2 * z + core, 2 * ((z + d) % 4) + core
                hop.append((src * cols_n + col, dst * cols_n + col))
        v_col = v_col + lax.ppermute(mine, ("rows", "cols"), hop)
    own_b1 = column_step("own", flag, [after(b1, v_row)], across_coef)
    own_b2 = column_step("own", flag, [after(b2, v_row)], across_coef)
    f_a1 = column_step("all", flag, [after(a1, v_row), got_a1, far_a1], across_coef)
    gram, v_col, own_b1, own_b2, f_a1, _ = lax.optimization_barrier(
        (gram, v_col, own_b1, own_b2, f_a1, far_a2)
    )
    sum_b2 = lax.ppermute(after(part_b2, gram), "cols", swap)

    weights = inverse(gram, obs_variance[None])
    f_a2 = column_step("all", flag, [a2, got_a2, far_a2], across_coef)
    right = dot_rows(weights, v_col)
    solved = jnp.sum(weights * innovation[None], axis=1)
    mean_band = lax.dynamic_slice_in_dim(field, 8 * r, 8, 0).reshape(-1)
    corrected = mean_band + jnp.sum(v_row * solved[None], axis=1)

    out = None
    for first_lat, terms in (
        (4, [own_b1, sum_b1]),
        (2, [f_a1]),
        (6, [own_b2, sum_b2]),
        (0, [f_a2]),
    ):
        out = correct(terms, v_row, right, first_lat, out)
    return (out, corrected)


def solution(mesh):
    return jax.shard_map(
        shards,
        mesh=mesh,
        in_specs=(P("rows", "cols"), P(), P(), P(), P(), P(), P(), P(), P()),
        out_specs=(P("rows", "cols"), P("rows")),
        check_vma=False,
    )
```
